32 devices in a mesh: site: 8 (over z, core), sector: 4 (over y, x).
Axes of the slice: x: 2, y: 2, z: 4, core: 2. Of those that a mesh axis runs over, the one named last changes fastest.
Arguments:
- site_tensor: float32 [8, 4, 16, 512, 512], P('site', None, 'sector'), may hold values from -0.25 to 0.25
- outcomes: int32 [6, 8, 128], P(None, 'site'), may hold values from 0 to 3
- in_flight: float32 [8, 128, 8192], P('site', None, 'sector'), may hold values from -6 to 6
- prior_logp: float32 [8, 128], P('site'), may hold values from -30 to 0
- entering: float32 [5, 128, 8192], P(None, None, 'sector'), may hold values from -6 to 6
Outputs:
- final_env: float32 [8, 128, 8192], P('site', None, 'sector')
- final_logp: float32 [8, 128], P('site')
The draws below stay inside these ranges and needn't reach their ends.
All inputs are finite; a program needn't handle non-finite values.
Results may differ from the reference program's by a relative error of at most 0.0003.
Values sent between devices are 32-bit elements; how exact they have to be, the bound alone decides.
No kernel may reach another device: no remote copies, remote signals or barrier semaphores. Data moves between devices by JAX's collectives and lax.ppermute only.
A program may use at most 64 MiB of HBM per device.

```python
import jax
import jax.numpy as jnp
from jax import lax

SECTORS = 16
SEC = 512
OUTCOMES = 4
ROWS = 128
TICKS = 6
BOND = 8192
SITES = 8
ENTERING = 5


def plant(array, own_key, smallest, high):
    longest = array.shape.index(max(array.shape))
    spots = []
    for shift in (0, 1):
        where = [jax.random.randint(jax.random.fold_in(own_key, axis), (), 0, length) for axis, length in enumerate(array.shape)]
        where[longest] = (where[longest] + shift) % array.shape[longest]
        spots.append(tuple(where))
    return array.at[spots[0]].set(smallest).at[spots[1]].set(high)


def block_levels(rng, shape, cuts, low, top_value):
    factor_of, own = 1.0, jax.random.fold_in(rng, 6)
    for axis_at, shards_of in cuts:
        draws = jnp.exp(jax.random.uniform(jax.random.fold_in(own, axis_at), (shards_of,), jnp.float32, low / len(cuts), top_value / len(cuts)))
        factor_of = factor_of * jnp.repeat(draws, shape[axis_at] // shards_of).reshape([-1 if axis == axis_at else 1 for axis in range(len(shape))])
    return factor_of


def noise(key, dims, deviation, most, pieces=(), held_as=jnp.bfloat16):
    entries = deviation * jax.random.normal(key, dims, jnp.float32)
    if pieces:
        entries = entries * block_levels(key, dims, pieces, -0.22, 0.18)
    return jnp.clip(entries, -most, most).astype(held_as)


def setup_inputs(seed: int = 0) -> dict:
    key_list = jax.random.split(jax.random.key(seed), 6)
    site_tensor = noise(key_list[0], (SITES, OUTCOMES, SECTORS, SEC, SEC), SEC ** -0.5, 0.25, ((0, 8), (2, 4)), jnp.float32)
    outcomes = plant(jax.random.randint(key_list[1], (TICKS, SITES, ROWS), 0, OUTCOMES), jax.random.fold_in(key_list[1], 1), 0, OUTCOMES - 1).astype(jnp.int32)
    in_flight = noise(key_list[2], (SITES, ROWS, BOND), 1.0, 6.0, ((0, 8), (2, 4)), jnp.float32)
    prior_logp = jnp.clip(-30.0 + 30.0 * jax.random.uniform(key_list[3], (SITES, ROWS), jnp.float32) ** block_levels(key_list[3], (SITES, ROWS), ((0, 8),), -0.2, 0.2), -30.0, 0.0)
    entering = noise(key_list[4], (ENTERING, ROWS, BOND), 1.0, 6.0, ((2, 4),), jnp.float32)
    return dict(site_tensor=site_tensor, outcomes=outcomes, in_flight=in_flight, prior_logp=prior_logp, entering=entering)


EPSILON = 1e-06

def reference(site_tensor, outcomes, in_flight, prior_logp, entering):

    def one_site(operands):
        tensor, states, log_weight, chosen = operands
        blocks = states.reshape(ROWS, SECTORS, SEC)
        padded = jnp.concatenate([blocks, jnp.zeros((ROWS, OUTCOMES - 1, SEC), dtype=states.dtype)], axis=1)
        picked = jnp.stack([padded[:, count:count + SECTORS] for count in range(OUTCOMES)], axis=1)
        amplitude = jnp.einsum('rnsi,nsij->rnsj', picked, tensor, precision=lax.Precision.HIGHEST)
        amplitude = amplitude.reshape(ROWS, OUTCOMES, BOND)
        power = lax.optimization_barrier(jnp.mean(amplitude * amplitude, axis=2))
        selector = (chosen[:, None] == jnp.arange(OUTCOMES, dtype=jnp.int32)[None, :]).astype(amplitude.dtype)
        picked_mean = lax.optimization_barrier(jnp.sum(power * selector, axis=1)) + EPSILON
        total_mean = lax.optimization_barrier(jnp.sum(power, axis=1)) + EPSILON
        selected = lax.optimization_barrier(jnp.sum(amplitude * selector[:, :, None], axis=1))
        normalized = selected / jnp.sqrt(picked_mean)[:, None]
        return (normalized, log_weight + jnp.log(picked_mean) - jnp.log(total_mean))
    states = in_flight
    log_weight = prior_logp
    for tick_index in range(TICKS):
        if tick_index > 0:
            states = jnp.concatenate([entering[tick_index - 1][None], states[:-1]], axis=0)
            log_weight = jnp.concatenate([jnp.zeros((1, ROWS), dtype=prior_logp.dtype), log_weight[:-1]], axis=0)
        states, log_weight = lax.map(one_site, (site_tensor, states, log_weight, outcomes[tick_index]))
    return (states, log_weight)
```

```python
import functools
import jax
import jax.numpy as jnp
from jax import lax
from jax.experimental import pallas as pl
from jax.experimental.pallas import tpu as pltpu
from jax.sharding import PartitionSpec as P

EPSILON = 1e-06
SCALE = 256.0
LANES = 128
CHUNKS = 2
BF = jnp.bfloat16
F32 = jnp.float32
AXES = ("site", "sector")


def split_kernel(w_ref, hi_ref, lo_ref):
    w = w_ref[...]
    hi = w.astype(BF)
    hi_ref[...] = hi
    lo_ref[...] = (w - hi.astype(F32)).astype(BF)


def split_weights(w):
    count, width, _ = w.shape
    spec = pl.BlockSpec((1, width, width), lambda i: (i, 0, 0))
    shape = jax.ShapeDtypeStruct(w.shape, BF)
    return pl.pallas_call(
        split_kernel,
        grid=(count,),
        in_specs=[spec],
        out_specs=[spec, spec],
        out_shape=[shape, shape],
        name="split_weights",
        cost_estimate=pl.CostEstimate(flops=w.size, bytes_accessed=8 * w.size, transcendentals=0),
    )(w)


def step_kernel(dims, tick, first, last, flags, *refs):
    n_out, local, width, rows, halo = dims
    refs = list(refs)
    choice_ref = refs.pop(0)
    main_ref = refs.pop(0)
    halo_refs = [refs.pop(0) for _ in halo]
    start_ref = None if first else refs.pop(0)
    next_ref = None if last else refs.pop(0)
    hi_ref, lo_ref = refs.pop(0), refs.pop(0)
    out_ref = refs.pop(0)
    part_ref = refs.pop(0) if last else None
    edge_ref = None if last else refs.pop(0)
    stack = refs.pop(0)
    s = pl.program_id(0)

    @pl.when(s == 0)
    def _():
        def put(index, value):
            hi = value.astype(BF)
            stack[index, :rows] = hi
            stack[index, rows:] = (value - hi.astype(F32)).astype(BF)

        for q in range(local):
            cols = slice(q * width, (q + 1) * width)
            if first:
                value = main_ref[:, cols] * SCALE
            else:
                value = jnp.where(flags[0] == 1, start_ref[:, cols] * SCALE, main_ref[:, cols])
            put(q, value)
        index = local
        for ref, blocks in zip(halo_refs, halo):
            for q in range(blocks):
                value = ref[:, q * width : (q + 1) * width]
                if first:
                    value = value * SCALE
                put(index, value)
                index += 1

    choice = choice_ref[:, tick : tick + 1]
    selected = None
    picked = jnp.zeros((rows, 1), F32)
    total = jnp.zeros((rows, 1), F32)
    for n in range(n_out):
        both = stack[s + n]
        top = both[:rows]
        wide = jnp.dot(both, hi_ref[n, 0], preferred_element_type=F32)
        value = wide[:rows] + wide[rows:]
        value = value + jnp.dot(top, lo_ref[n, 0], preferred_element_type=F32)
        power = jnp.sum(value * value, axis=1, keepdims=True)
        mine = choice == n
        total = total + power
        picked = jnp.where(mine, power, picked)
        selected = jnp.where(mine, value, 0.0) if n == 0 else jnp.where(mine, value, selected)
    base = pl.multiple_of(s * width, LANES)
    out_ref[:, pl.ds(base, width)] = selected
    if not last:
        for q in range(halo[0]):

            @pl.when(s == q)
            def _():
                cols = slice(q * width, (q + 1) * width)
                edge_ref[:, cols] = jnp.where(flags[1] == 1, next_ref[:, cols] * SCALE, selected)

    lane = lax.broadcasted_iota(jnp.int32, (rows, LANES), 1)
    new = jnp.where(lane == 2 * tick, picked, jnp.where(lane == 2 * tick + 1, total, 0.0))
    dest = part_ref if last else out_ref
    where = slice(None) if last else slice(local * width, local * width + LANES)

    @pl.when(s == 0)
    def _():
        if first:
            old = jnp.zeros((rows, LANES), F32)
        else:
            old = main_ref[:, local * width : local * width + LANES]
            old = jnp.where(flags[0] == 1, 0.0, old)
        dest[:, where] = old + new

    @pl.when(s > 0)
    def _():
        dest[:, where] = dest[:, where] + new


def step(dims, tick, ticks, flags, choice, main, halos, entering, chunk, weights):
    n_out, local, width, rows, halo = dims
    first, last = tick == 0, tick == ticks - 1
    span = local * width
    whole = lambda shape: pl.BlockSpec(shape, lambda s, f: (0,) * len(shape))
    row_block = lambda cols: pl.BlockSpec((rows, cols), lambda s, f: (chunk, 0))
    operands = [choice, main]
    specs = [row_block(choice.shape[1])]
    if first:
        specs.append(row_block(span))
    else:
        specs.append(whole(main.shape))
    for value in halos:
        operands.append(value)
        specs.append(whole(value.shape))
    if not first:
        operands.append(entering)
        specs.append(pl.BlockSpec((None, rows, span), lambda s, f, t=tick - 1: (t, chunk, 0)))
    if not last:
        operands.append(entering)
        specs.append(pl.BlockSpec((None, rows, halo[0] * width), lambda s, f, t=tick: (t, chunk, 0)))
    for value in weights:
        operands.append(value)
        specs.append(pl.BlockSpec((n_out, 1, width, width), lambda s, f: (0, s, 0, 0)))
    if last:
        shapes = [(rows, span), (rows, LANES)]
    else:
        shapes = [(rows, span + LANES), (rows, halo[0] * width)]
    blocks = local + sum(halo)
    return pl.pallas_call(
        functools.partial(step_kernel, dims, tick, first, last),
        grid_spec=pltpu.PrefetchScalarGridSpec(
            num_scalar_prefetch=1,
            grid=(local,),
            in_specs=specs,
            out_specs=[whole(shape) for shape in shapes],
            scratch_shapes=[pltpu.VMEM((blocks, 2 * rows, width), BF)],
        ),
        out_shape=[jax.ShapeDtypeStruct(shape, F32) for shape in shapes],
        name=f"step_{tick}_{chunk}",
        cost_estimate=pl.CostEstimate(
            flops=6 * rows * n_out * local * width * width,
            bytes_accessed=4 * n_out * local * width * width,
            transcendentals=0,
        ),
    )(flags, *operands)


def final_kernel(ticks, bond, chunks, *refs):
    state_refs = refs[:chunks]
    part_refs = refs[chunks : 2 * chunks]
    prior_ref, env_ref, logp_ref = refs[2 * chunks :]
    rows = state_refs[0].shape[0]
    scale = 1.0 / (bond * SCALE * SCALE)
    for c in range(chunks):
        sums = part_refs[c][...].T * scale
        own = slice(c * rows, (c + 1) * rows)
        log_weight = prior_ref[:, own]
        factor = jnp.ones((1, rows), F32)
        for t in range(ticks):
            picked = sums[2 * t : 2 * t + 1] * factor * factor + EPSILON
            total = sums[2 * t + 1 : 2 * t + 2] * factor * factor + EPSILON
            log_weight = log_weight + jnp.log(picked) - jnp.log(total)
            factor = factor * lax.rsqrt(picked)
        logp_ref[:, own] = log_weight
        column = jnp.broadcast_to(factor, (LANES, rows)).T[:, :1]
        env_ref[0, own] = state_refs[c][...] * (column * (1.0 / SCALE))


def finish(states, parts, prior, ticks, bond):
    rows = sum(value.shape[0] for value in states)
    span = states[0].shape[1]
    return pl.pallas_call(
        functools.partial(final_kernel, ticks, float(bond), len(states)),
        out_shape=[
            jax.ShapeDtypeStruct((1, rows, span), F32),
            jax.ShapeDtypeStruct((1, rows), F32),
        ],
        name="finish",
    )(*states, *parts, prior)


def per_device(sites, sectors, site_tensor, outcomes, in_flight, prior_logp, entering):
    weights = site_tensor[0]
    n_out, local, width = weights.shape[:3]
    span = in_flight.shape[2]
    total_rows = in_flight.shape[1]
    ticks = outcomes.shape[0]
    rows = total_rows // CHUNKS
    need = n_out - 1
    halo = []
    while need > 0:
        halo.append(min(local, need))
        need -= halo[-1]
    dims = (n_out, local, width, rows, tuple(halo))
    place = lambda k, d: k * sectors + d
    main_pairs = [(place(k, d), place(k + 1, d)) for k in range(sites - 1) for d in range(sectors)]

    def halo_pairs(hop, shift):
        return [
            (place(k, d + hop), place((k + shift) % sites, d))
            for k in range(sites)
            for d in range(sectors - hop)
        ]

    def halo_moved(edge, shift):
        return [
            lax.ppermute(edge[:, : blocks * width], AXES, halo_pairs(hop + 1, shift))
            for hop, blocks in enumerate(halo)
        ]

    site = lax.axis_index("site")
    flags = jnp.stack([site == 0, site == sites - 1]).astype(jnp.int32)
    choice = outcomes[:, 0].T
    prior = lax.ppermute(
        prior_logp, "site", [(k, k + ticks - 1) for k in range(sites - ticks + 1)]
    )
    halos = [
        halo_moved(in_flight[0, c * rows : (c + 1) * rows, : halo[0] * width], 0)
        for c in range(CHUNKS)
    ]
    split = split_weights(weights.reshape(n_out * local, width, width))
    split = [value.reshape(weights.shape) for value in split]
    mains = [in_flight[0]] * CHUNKS
    parts = [None] * CHUNKS
    for tick in range(ticks):
        for c in range(CHUNKS):
            main, other = step(
                dims, tick, ticks, flags, choice, mains[c], halos[c], entering, c, split
            )
            if tick < ticks - 1:
                mains[c] = lax.ppermute(main, AXES, main_pairs)
                halos[c] = halo_moved(other, 1)
            else:
                mains[c] = main
                parts[c] = lax.psum(other, "sector")
    return tuple(finish(mains, parts, prior, ticks, span * sectors))


def solution(mesh):
    sizes = (mesh.shape["site"], mesh.shape["sector"])
    return jax.shard_map(
        functools.partial(per_device, *sizes),
        mesh=mesh,
        in_specs=(
            P("site", None, "sector", None, None),
            P(None, "site", None),
            P("site", None, "sector"),
            P("site", None),
            P(None, None, "sector"),
        ),
        out_specs=(P("site", None, "sector"), P("site", None)),
        check_vma=False,
    )
```

```python
import functools
import jax
import jax.numpy as jnp
from jax import lax
from jax.experimental import pallas as pl
from jax.experimental.pallas import tpu as pltpu
from jax.sharding import PartitionSpec as P


EPSILON = 1e-06
SCALE = 256.0
LANES = 128
CHUNKS = 2
BF = jnp.bfloat16
F32 = jnp.float32
AXES = ("site", "sector")
VMEM_SPEC = pl.BlockSpec(memory_space=pltpu.VMEM)
VMEM_LIMIT = 8 << 20
UNROLL = 2


def in_vmem(value):
    return pltpu.with_memory_space_constraint(value, pltpu.VMEM)


def split_kernel(w_ref, hi_ref, lo_ref, buffer, sems):
    count, depth = w_ref.shape[0], buffer.shape[0]
    copies = [
        pltpu.make_async_copy(w_ref.at[i], buffer.at[i % depth], sems.at[i % depth])
        for i in range(count)
    ]
    for copy in copies[:depth]:
        copy.start()
    for i in range(count):
        copies[i].wait()
        w = buffer[i % depth]
        hi = w.astype(BF)
        hi_ref[i] = hi
        lo_ref[i] = (w - hi.astype(F32)).astype(BF)
        if i + depth < count:
            copies[i + depth].start()


def split_weights(w):
    count, width, _ = w.shape
    depth = min(4, count)
    return pl.pallas_call(
        split_kernel,
        in_specs=[pl.BlockSpec(memory_space=pl.ANY)],
        out_specs=[VMEM_SPEC] * 2,
        out_shape=[pltpu.VMEM(w.shape, BF)] * 2,
        scratch_shapes=[
            pltpu.VMEM((depth, width, width), F32),
            pltpu.SemaphoreType.DMA((depth,)),
        ],
        compiler_params=pltpu.CompilerParams(vmem_limit_bytes=(4 * depth + 2) * width * width),
        name="split_weights",
        cost_estimate=pl.CostEstimate(flops=w.size, bytes_accessed=8 * w.size, transcendentals=0),
    )(w)


def step_kernel(dims, tick, ticks, chunk, *refs):
    n_out, local, width, rows, halo = dims
    first, last = tick == 0, tick == ticks - 1
    span = local * width
    refs = list(refs)
    flag_ref = refs.pop(0)
    choice_ref = refs.pop(0)
    main_ref = refs.pop(0)
    halo_refs = [refs.pop(0) for _ in halo]
    entering_ref = refs.pop(0)
    hi_ref, lo_ref = refs.pop(0), refs.pop(0)
    out_ref = refs.pop(0)
    part_ref = refs.pop(0) if last else None
    edge_ref = None if last else refs.pop(0)
    stack = refs.pop(0)
    own = slice(chunk * rows, (chunk + 1) * rows)
    at_start = flag_ref[0] == 1
    at_end = flag_ref[1] == 1

    def put(index, value):
        hi = value.astype(BF)
        stack[index, :rows] = hi
        stack[index, rows:] = (value - hi.astype(F32)).astype(BF)

    for q in range(local):
        cols = slice(q * width, (q + 1) * width)
        if first:
            value = main_ref[0, own, cols] * SCALE
        else:
            value = jnp.where(at_start, entering_ref[tick - 1, own, cols] * SCALE, main_ref[:, cols])
        put(q, value)
    index = local
    for ref, blocks in zip(halo_refs, halo):
        for q in range(blocks):
            value = ref[:, q * width : (q + 1) * width]
            put(index, value * SCALE if first else value)
            index += 1

    choice = choice_ref[own, tick : tick + 1]

    def column(s, carry):
        picked, total = carry
        selected = None
        for n in range(n_out):
            both = stack[s + n]
            wide = jnp.dot(both, hi_ref[n, s], preferred_element_type=F32)
            value = wide[:rows] + wide[rows:]
            value = value + jnp.dot(both[:rows], lo_ref[n, s], preferred_element_type=F32)
            power = jnp.sum(value * value, axis=1, keepdims=True)
            mine = choice == n
            total = total + power
            picked = picked + jnp.where(mine, power, 0.0)
            selected = jnp.where(mine, value, 0.0 if n == 0 else selected)
        out_ref[:, pl.ds(pl.multiple_of(s * width, width), width)] = selected
        return picked, total

    zero = jnp.zeros((rows, 1), F32)
    picked, total = lax.fori_loop(0, local, column, (zero, zero), unroll=min(UNROLL, local))
    if not last:
        for q in range(halo[0]):
            cols = slice(q * width, (q + 1) * width)
            own_rows = entering_ref[tick, own, cols] * SCALE
            edge_ref[:, cols] = jnp.where(at_end, own_rows, out_ref[:, cols])

    lane = lax.broadcasted_iota(jnp.int32, (rows, LANES), 1)
    sums = jnp.where(lane == 2 * tick, picked, jnp.where(lane == 2 * tick + 1, total, 0.0))
    if not first:
        sums = sums + jnp.where(at_start, 0.0, main_ref[:, span : span + LANES])
    if last:
        part_ref[...] = sums
    else:
        out_ref[:, span : span + LANES] = sums


def step(dims, tick, ticks, chunk, flags, choice, main, halos, entering, weights):
    n_out, local, width, rows, halo = dims
    last = tick == ticks - 1
    span = local * width
    operands = [choice, main, *halos, entering, *weights]
    if last:
        shapes = [(rows, span), (rows, LANES)]
    else:
        shapes = [(rows, span + LANES), (rows, halo[0] * width)]
    blocks = local + sum(halo)
    return pl.pallas_call(
        functools.partial(step_kernel, dims, tick, ticks, chunk),
        in_specs=[pl.BlockSpec(memory_space=pltpu.SMEM)] + [VMEM_SPEC] * len(operands),
        out_specs=[VMEM_SPEC] * 2,
        out_shape=[pltpu.VMEM(shape, F32) for shape in shapes],
        scratch_shapes=[pltpu.VMEM((blocks, 2 * rows, width), BF)],
        compiler_params=pltpu.CompilerParams(vmem_limit_bytes=VMEM_LIMIT),
        cost_estimate=pl.CostEstimate(
            flops=6 * rows * n_out * local * width * width,
            bytes_accessed=4 * rows * span,
            transcendentals=0,
        ),
    )(flags, *[in_vmem(value) for value in operands])


def final_kernel(ticks, bond, chunks, copies, *refs):
    refs = list(refs)
    state_refs = [refs.pop(0) for _ in range(chunks)]
    part_refs = [[refs.pop(0) for _ in range(copies)] for _ in range(chunks)]
    prior_ref, env_ref, logp_ref = refs
    rows = state_refs[0].shape[0]
    scale = 1.0 / (bond * SCALE * SCALE)
    for c in range(chunks):
        sums = [ref[...] for ref in part_refs[c]]
        while len(sums) > 1:
            sums = [sums[i] + sums[i + 1] for i in range(0, len(sums), 2)]
        sums = sums[0].T * scale
        own = slice(c * rows, (c + 1) * rows)
        log_weight = prior_ref[:, own]
        factor = jnp.ones((1, rows), F32)
        for t in range(ticks):
            picked = sums[2 * t : 2 * t + 1] * factor * factor + EPSILON
            total = sums[2 * t + 1 : 2 * t + 2] * factor * factor + EPSILON
            log_weight = log_weight + jnp.log(picked) - jnp.log(total)
            factor = factor * lax.rsqrt(picked)
        logp_ref[:, own] = log_weight
        column = jnp.broadcast_to(factor, (LANES, rows)).T[:, :1]
        env_ref[0, own] = state_refs[c][...] * (column * (1.0 / SCALE))


def finish(states, parts, prior, ticks, bond):
    rows = sum(value.shape[0] for value in states)
    span = states[0].shape[1]
    operands = [*states, *[value for group in parts for value in group], prior]
    return pl.pallas_call(
        functools.partial(final_kernel, ticks, float(bond), len(states), len(parts[0])),
        in_specs=[VMEM_SPEC] * len(operands),
        out_shape=[
            jax.ShapeDtypeStruct((1, rows, span), F32),
            jax.ShapeDtypeStruct((1, rows), F32),
        ],
        compiler_params=pltpu.CompilerParams(vmem_limit_bytes=VMEM_LIMIT),
        name="finish",
    )(*operands)


def sector_terms(value, sectors):
    if sectors & (sectors - 1) or sectors == 1:
        return [lax.psum(value, "sector")]
    if sectors <= 4:
        return [value] + [
            lax.ppermute(value, "sector", [(d, d ^ mask) for d in range(sectors)])
            for mask in range(1, sectors)
        ]
    mask = 1
    while 2 * mask < sectors:
        value = value + lax.ppermute(value, "sector", [(d, d ^ mask) for d in range(sectors)])
        mask *= 2
    return [value, lax.ppermute(value, "sector", [(d, d ^ mask) for d in range(sectors)])]


def per_device(sites, sectors, site_tensor, outcomes, in_flight, prior_logp, entering):
    weights = site_tensor[0]
    n_out, local, width = weights.shape[:3]
    span = in_flight.shape[2]
    total_rows = in_flight.shape[1]
    ticks = outcomes.shape[0]
    rows = total_rows // CHUNKS
    need = n_out - 1
    halo = []
    while need > 0:
        halo.append(min(local, need))
        need -= halo[-1]
    dims = (n_out, local, width, rows, tuple(halo))
    place = lambda k, d: k * sectors + d
    main_pairs = [(place(k, d), place(k + 1, d)) for k in range(sites - 1) for d in range(sectors)]

    def halo_pairs(hop, shift):
        return [
            (place(k, d + hop), place((k + shift) % sites, d))
            for k in range(sites)
            for d in range(sectors - hop)
        ]

    def halo_moved(edge, shift):
        moved = []
        for hop, blocks in enumerate(halo):
            moved.append(lax.ppermute(edge[:, : blocks * width], AXES, halo_pairs(hop + 1, shift)))
        return moved

    site = lax.axis_index("site")
    flags = jnp.stack([site == 0, site == sites - 1]).astype(jnp.int32)
    choice = outcomes[:, 0].T
    prior = lax.ppermute(
        prior_logp, "site", [(k, k + ticks - 1) for k in range(sites - ticks + 1)]
    )
    halos = [
        halo_moved(in_flight[0, c * rows : (c + 1) * rows, : halo[0] * width], 0)
        for c in range(CHUNKS)
    ]
    split = split_weights(weights.reshape(n_out * local, width, width))
    split = [value.reshape(weights.shape) for value in split]
    mains = [in_flight] * CHUNKS
    parts = [None] * CHUNKS
    for tick in range(ticks):
        for c in range(CHUNKS):
            main, other = step(
                dims, tick, ticks, c, flags, choice, mains[c], halos[c], entering, split
            )
            if tick < ticks - 1:
                halos[c] = halo_moved(other, 1)
                mains[c] = lax.ppermute(main, AXES, main_pairs)
            else:
                mains[c] = main
                parts[c] = sector_terms(other, sectors)
    return tuple(finish(mains, parts, prior, ticks, span * sectors))


def solution(mesh):
    sizes = (mesh.shape["site"], mesh.shape["sector"])

    def whole(site_tensor, outcomes, *others):
        call = jax.shard_map(
            functools.partial(per_device, *sizes),
            mesh=mesh,
            in_specs=(
                P("site", None, "sector", None, None),
                P(None, "site", None),
                P("site", None, "sector"),
                P("site", None),
                P(None, None, "sector"),
            ),
            out_specs=(P("site", None, "sector"), P("site", None)),
            check_vma=False,
        )
        return call(site_tensor, outcomes, *others)

    return whole
```

```python
import functools

import jax
import jax.numpy as jnp
from jax import lax
from jax.experimental import pallas as pl
from jax.experimental.pallas import tpu as pltpu
from jax.sharding import PartitionSpec as P


EPSILON = 1e-06
SCALE = 256.0
LANES = 128
CHUNKS = 2
BUFFERS = 8
VMEM_LIMIT = 12 << 20
BF = jnp.bfloat16
F32 = jnp.float32
VMEM_SPEC = pl.BlockSpec(memory_space=pltpu.VMEM)


def sums_depth(ticks):
    return -(-(2 * ticks + 1) // 8) * 8


def in_vmem(value):
    return pltpu.with_memory_space_constraint(value, pltpu.VMEM)


def put(stack, index, start, value):
    rows, cols = value.shape
    hi = value.astype(BF)
    stack[index, :rows, start : start + cols] = hi
    stack[index, rows:, start : start + cols] = (value - hi.astype(F32)).astype(BF)


def product(both, hi, lo):
    rows = both.shape[0] // 2
    wide = jnp.dot(both, hi, preferred_element_type=F32)
    value = wide[:rows] + wide[rows:]
    return value + jnp.dot(both[:rows], lo, preferred_element_type=F32)


def folded_squares(value):
    square = value * value
    total = square[:, :LANES]
    for start in range(LANES, square.shape[1], LANES):
        total = total + square[:, start : start + LANES]
    return total


def as_row(index, squares, depth):
    rows = squares.shape[0]
    lane = lax.broadcasted_iota(jnp.int32, (rows, LANES), 1)
    column = jnp.sum(squares, axis=1, keepdims=True)
    return jnp.where(lane == index, column, 0.0).T[:depth]


def open_kernel(dims, ticks, flag_ref, w_ref, rows_ref, outcome_ref, prior_ref, *rest):
    hi_ref, lo_ref, out_ref, sums_ref, choice_ref, *rest = rest
    stack, buffer, row_buffer, outcome_buffer, prior_buffer, sems = rest
    n_out, local, width, _, _ = dims
    rows = rows_ref.shape[1]
    depth, count = buffer.shape[0], n_out * local
    order = [(n, s) for s in range(local) for n in range(n_out)]
    copies = [
        pltpu.make_async_copy(w_ref.at[n, s], buffer.at[i % depth], sems.at[i % depth])
        for i, (n, s) in enumerate(order)
    ]
    inputs = [
        pltpu.make_async_copy(outcome_ref, outcome_buffer, sems.at[depth]),
        pltpu.make_async_copy(rows_ref, row_buffer, sems.at[depth + 1]),
        pltpu.make_async_copy(prior_ref, prior_buffer, sems.at[depth + 2]),
    ]
    for copy in inputs:
        copy.start()
    for copy in copies[:depth]:
        copy.start()
    for copy in inputs:
        copy.wait()
    outcomes = outcome_buffer[:, 0].astype(F32)
    padding = jnp.zeros((LANES - outcomes.shape[0], rows), F32)
    choice_ref[...] = jnp.concatenate([outcomes, padding], axis=0).T
    choice = choice_ref[:, :1]
    for q in range(local):
        put(stack, q, 0, row_buffer[0, :, q * width : (q + 1) * width] * SCALE)
    total = jnp.zeros((rows, LANES), F32)
    selected = None
    for i, (n, s) in enumerate(order):
        copies[i].wait()
        w = buffer[i % depth]
        hi = w.astype(BF)
        lo = (w - hi.astype(F32)).astype(BF)
        hi_ref[n, s] = hi
        lo_ref[n, s] = lo
        if s + n < local:
            value = product(stack[s + n], hi, lo)
            total = total + folded_squares(value)
            selected = jnp.where(choice == n, value, 0.0 if n == 0 else selected)
        if i + depth < count:
            copies[i + depth].start()
        if n == n_out - 1:
            out_ref[:, s * width : (s + 1) * width] = selected
    depth = sums_ref.shape[0]
    row = lax.broadcasted_iota(jnp.int32, (depth, rows), 0)
    prior = jnp.where(flag_ref[2] == 1, jnp.broadcast_to(prior_buffer[...], (depth, rows)), 0.0)
    sums_ref[...] = as_row(1, total, depth) + jnp.where(row == 2 * ticks, prior, 0.0)


def opened(dims, ticks, flags, weights, in_flight, outcomes, prior):
    n_out, local, width, _, _ = dims
    rows = in_flight.shape[1]
    depth = min(BUFFERS, n_out * local)
    operands = [weights, in_flight, outcomes, prior]
    return pl.pallas_call(
        functools.partial(open_kernel, dims, ticks),
        in_specs=[pl.BlockSpec(memory_space=pltpu.SMEM)]
        + [pl.BlockSpec(memory_space=pltpu.HBM)] * len(operands),
        out_specs=[VMEM_SPEC] * 5,
        out_shape=[
            pltpu.VMEM(weights.shape, BF),
            pltpu.VMEM(weights.shape, BF),
            pltpu.VMEM((rows, local * width), F32),
            pltpu.VMEM((sums_depth(ticks), rows), F32),
            pltpu.VMEM((rows, LANES), F32),
        ],
        scratch_shapes=[
            pltpu.VMEM((local, 2 * rows, width), BF),
            pltpu.VMEM((depth, width, width), F32),
            pltpu.VMEM(in_flight.shape, F32),
            pltpu.VMEM(outcomes.shape, jnp.int32),
            pltpu.VMEM(prior.shape, F32),
            pltpu.SemaphoreType.DMA((depth + 3,)),
        ],
        compiler_params=pltpu.CompilerParams(vmem_limit_bytes=2 * VMEM_LIMIT),
        name="opened",
        cost_estimate=pl.CostEstimate(
            flops=3 * rows * n_out * local * width * width,
            bytes_accessed=4 * weights.size,
            transcendentals=0,
        ),
    )(flags, *[pltpu.with_memory_space_constraint(value, pltpu.HBM) for value in operands])


def near_kernel(dims, tick, chunk, *refs):
    flag_ref, choice_ref, hi_ref, lo_ref, main_ref, entering_ref, out_ref, sums_ref, stack = refs
    n_out, local, width, rows, _ = dims
    own = slice(chunk * rows, (chunk + 1) * rows)
    at_start = flag_ref[0] == 1
    group = 0
    for q in range(local):
        for start in range(0, width, LANES):
            cols = slice(q * width + start, q * width + start + LANES)
            fresh = entering_ref[tick - 1, own, cols] * SCALE
            value = main_ref[group * rows : (group + 1) * rows]
            put(stack, q, start, jnp.where(at_start, fresh, value))
            group += 1
    choice = choice_ref[own, tick : tick + 1]
    total = jnp.zeros((rows, LANES), F32)
    for s in range(local):
        selected = None
        for n in range(min(n_out, local - s)):
            value = product(stack[s + n], hi_ref[n, s], lo_ref[n, s])
            total = total + folded_squares(value)
            selected = jnp.where(choice == n, value, 0.0 if n == 0 else selected)
        out_ref[:, s * width : (s + 1) * width] = selected
    depth = sums_ref.shape[0]
    old = main_ref[group * rows :, :rows]
    sums_ref[...] = jnp.where(at_start, 0.0, old) + as_row(2 * tick + 1, total, depth)


def far_kernel(dims, tick, ticks, chunk, *refs):
    n_out, local, width, rows, halo = dims
    last = tick == ticks - 1
    refs = list(refs)
    flag_ref, choice_ref, hi_ref, lo_ref, base_ref, base_sums_ref = refs[:6]
    halo_refs = refs[6 : 6 + len(halo)]
    other_refs, stack = refs[6 + len(halo) : -1], refs[-1]
    own = slice(chunk * rows, (chunk + 1) * rows)
    base = slice(None) if base_ref.shape[0] == rows else own
    index = local
    for ref, blocks in zip(halo_refs, halo):
        for q in range(blocks):
            value = ref[:, q * width : (q + 1) * width]
            put(stack, index, 0, value * SCALE if tick == 0 else value)
            index += 1
    if last:
        *done_refs, out_ref, part_ref = other_refs
    else:
        entering_ref, out_ref, edge_ref = other_refs
    at_end = flag_ref[1] == 1
    choice = choice_ref[own, tick : tick + 1]
    total = jnp.zeros((rows, LANES), F32)
    picked = jnp.zeros((rows, LANES), F32)
    for s in range(local):
        cols = slice(s * width, (s + 1) * width)
        selected = base_ref[base, cols]
        for n in range(max(0, local - s), n_out):
            value = product(stack[s + n], hi_ref[n, s], lo_ref[n, s])
            total = total + folded_squares(value)
            selected = jnp.where(choice == n, value, selected)
        picked = picked + folded_squares(selected)
        if last:
            out_ref[:, cols] = selected
            continue
        for start in range(0, width, LANES):
            at = (s * width + start) // LANES * rows
            out_ref[at : at + rows] = selected[:, start : start + LANES]
        if s < halo[0]:
            fresh = entering_ref[tick, own, cols] * SCALE
            edge_ref[:, cols] = jnp.where(at_end, fresh, selected)
    depth = base_sums_ref.shape[0]
    sums = base_sums_ref[:, base] + as_row(2 * tick + 1, total, depth)
    sums = sums + as_row(2 * tick, picked, depth)
    if last:
        for ref in done_refs:
            part_ref[:, : chunk * rows] = ref[:, : chunk * rows]
        part_ref[:, own] = sums
    else:
        out_ref[local * width // LANES * rows :, :rows] = sums


def step(kernel, dims, blocks, count, outs, operands):
    _, local, width, rows, _ = dims
    flags, *values = operands
    return pl.pallas_call(
        kernel,
        in_specs=[pl.BlockSpec(memory_space=pltpu.SMEM)] + [VMEM_SPEC] * len(values),
        out_specs=[VMEM_SPEC] * len(outs),
        out_shape=[pltpu.VMEM(shape, F32) for shape in outs],
        scratch_shapes=[pltpu.VMEM((blocks, 2 * rows, width), BF)],
        compiler_params=pltpu.CompilerParams(vmem_limit_bytes=VMEM_LIMIT),
        cost_estimate=pl.CostEstimate(
            flops=6 * rows * count * width * width,
            bytes_accessed=4 * rows * local * width,
            transcendentals=0,
        ),
    )(flags, *[in_vmem(value) for value in values])


def near(dims, tick, ticks, chunk, shared, main, entering):
    n_out, local, width, rows, _ = dims
    count = sum(s + n < local for s in range(local) for n in range(n_out))
    outs = [(rows, local * width), (sums_depth(ticks), rows)]
    kernel = functools.partial(near_kernel, dims, tick, chunk)
    operands = [*shared, main, entering]
    return step(kernel, dims, local, count, outs, operands)


def far(dims, tick, ticks, chunk, shared, state, halos, entering, done):
    n_out, local, width, rows, halo = dims
    count = sum(s + n >= local for s in range(local) for n in range(n_out))
    depth = sums_depth(ticks)
    if tick == ticks - 1:
        outs = [(rows, local * width), (depth, CHUNKS * rows)]
        others = done
    else:
        outs = [(local * width // LANES * rows + depth, LANES), (rows, halo[0] * width)]
        others = [entering]
    kernel = functools.partial(far_kernel, dims, tick, ticks, chunk)
    operands = [*shared, *state, *halos, *others]
    blocks = local + sum(halo)
    return step(kernel, dims, blocks, count, outs, operands)


def final_kernel(ticks, bond, chunks, copies, *refs):
    state_refs = refs[:chunks]
    part_refs = refs[chunks : chunks + copies]
    env_ref, logp_ref = refs[chunks + copies :]
    rows = state_refs[0].shape[0]
    sums = [ref[...] for ref in part_refs]
    while len(sums) > 1:
        sums = [sums[i] + sums[i + 1] for i in range(0, len(sums), 2)]
    log_weight = sums[0][2 * ticks : 2 * ticks + 1]
    sums = sums[0] * (1.0 / (bond * SCALE * SCALE))
    factor = jnp.ones_like(log_weight)
    for t in range(ticks):
        picked = sums[2 * t : 2 * t + 1] * factor * factor + EPSILON
        total = sums[2 * t + 1 : 2 * t + 2] * factor * factor + EPSILON
        log_weight = log_weight + jnp.log(picked) - jnp.log(total)
        factor = factor * lax.rsqrt(picked)
    logp_ref[...] = log_weight
    column = jnp.broadcast_to(factor * (1.0 / SCALE), (LANES, factor.shape[1])).T[:, :1]
    for c in range(chunks):
        own = slice(c * rows, (c + 1) * rows)
        env_ref[0, own] = state_refs[c][...] * column[own]


def finish(states, parts, ticks, bond):
    rows = sum(value.shape[0] for value in states)
    span = states[0].shape[1]
    operands = [*states, *parts]
    return pl.pallas_call(
        functools.partial(final_kernel, ticks, float(bond), len(states), len(parts)),
        in_specs=[VMEM_SPEC] * len(operands),
        out_shape=[
            jax.ShapeDtypeStruct((1, rows, span), F32),
            jax.ShapeDtypeStruct((1, rows), F32),
        ],
        compiler_params=pltpu.CompilerParams(vmem_limit_bytes=VMEM_LIMIT),
        name="finish",
    )(*[in_vmem(value) for value in operands])


def sector_terms(value, sectors):
    if sectors & (sectors - 1) or sectors == 1:
        return [lax.psum(value, "sector")]

    def partner(term, mask):
        return lax.ppermute(term, "sector", [(d, d ^ mask) for d in range(sectors)])

    if sectors <= 4:
        return [value] + [partner(value, mask) for mask in range(1, sectors)]
    mask = 1
    while 2 * mask < sectors:
        value = value + partner(value, mask)
        mask *= 2
    return [value, partner(value, mask)]


def per_device(sites, sectors, site_tensor, outcomes, in_flight, prior_logp, entering):
    weights = site_tensor[0]
    n_out, local, width = weights.shape[:3]
    span = in_flight.shape[2]
    ticks = outcomes.shape[0]
    rows = in_flight.shape[1] // CHUNKS
    need = n_out - 1
    halo = []
    while need > 0:
        halo.append(min(local, need))
        need -= halo[-1]
    dims = (n_out, local, width, rows, tuple(halo))
    up = [(k, k + 1) for k in range(sites - 1)]

    def moved(edge, shift):
        pieces = []
        for hop, blocks in enumerate(halo):
            pairs = [
                (k * sectors + d + hop + 1, (k + shift) % sites * sectors + d)
                for k in range(sites)
                for d in range(sectors - hop - 1)
            ]
            pieces.append(lax.ppermute(edge[:, : blocks * width], ("site", "sector"), pairs))
        return pieces

    site = lax.axis_index("site")
    flags = [site == 0, site == sites - 1, lax.axis_index("sector") == 0]
    flags = jnp.stack(flags).astype(jnp.int32)
    halos = [
        moved(in_flight[0, c * rows : (c + 1) * rows, : halo[0] * width], 0)
        for c in range(CHUNKS)
    ]
    hi, lo, base, base_sums, choice = opened(
        dims, ticks, flags, weights, in_flight, outcomes, prior_logp
    )
    shared = [flags, choice, hi, lo]
    states = [(base, base_sums)] * CHUNKS
    mains = [None] * CHUNKS
    done = []
    for tick in range(ticks):
        for c in range(CHUNKS):
            if tick > 0:
                states[c] = near(dims, tick, ticks, c, shared, mains[c], entering)
            mains[c], other = far(dims, tick, ticks, c, shared, states[c], halos[c], entering, done)
            if tick == ticks - 1:
                done = [other]
                continue
            mains[c] = lax.ppermute(mains[c], "site", up)
            halos[c] = moved(other, 1)
    parts = sector_terms(done[0], sectors)
    return tuple(finish(mains, parts, ticks, span * sectors))


def solution(mesh):
    sizes = (mesh.shape["site"], mesh.shape["sector"])

    def whole(site_tensor, outcomes, *others):
        call = jax.shard_map(
            functools.partial(per_device, *sizes),
            mesh=mesh,
            in_specs=(
                P("site", None, "sector", None, None),
                P(None, "site", None),
                P("site", None, "sector"),
                P("site", None),
                P(None, None, "sector"),
            ),
            out_specs=(P("site", None, "sector"), P("site", None)),
            check_vma=False,
        )
        return call(site_tensor, outcomes, *others)

    return whole
```

```python
import functools

import jax
import jax.numpy as jnp
from jax import lax
from jax.experimental import pallas as pl
from jax.experimental.pallas import tpu as pltpu
from jax.sharding import PartitionSpec as P


EPSILON = 1e-06
SCALE = 256.0
LANES = 128
CHUNKS = 2
BUFFERS = 8
VMEM_LIMIT = 12 << 20
BF = jnp.bfloat16
F32 = jnp.float32
VMEM_SPEC = pl.BlockSpec(memory_space=pltpu.VMEM)


def sums_depth(ticks):
    return -(-(2 * ticks + 1) // 8) * 8


def in_vmem(value):
    return pltpu.with_memory_space_constraint(value, pltpu.VMEM)


def put(stack, index, start, value):
    rows, cols = value.shape
    hi = value.astype(BF)
    stack[index, :rows, start : start + cols] = hi
    stack[index, rows:, start : start + cols] = (value - hi.astype(F32)).astype(BF)


def product(both, hi, lo):
    rows = both.shape[0] // 2
    wide = jnp.dot(both, hi, preferred_element_type=F32)
    value = wide[:rows] + wide[rows:]
    return value + jnp.dot(both[:rows], lo, preferred_element_type=F32)


def folded_squares(value):
    square = value * value
    total = square[:, :LANES]
    for start in range(LANES, square.shape[1], LANES):
        total = total + square[:, start : start + LANES]
    return total


def as_row(index, squares, depth):
    rows = squares.shape[0]
    lane = lax.broadcasted_iota(jnp.int32, (rows, LANES), 1)
    column = jnp.sum(squares, axis=1, keepdims=True)
    return jnp.where(lane == index, column, 0.0).T[:depth]


def edge_kernel(rows_ref, *rest):
    *edge_refs, sems = rest
    rows, cols = edge_refs[0].shape
    copies = [
        pltpu.make_async_copy(
            rows_ref.at[0, pl.ds(c * rows, rows), pl.ds(0, cols)], ref, sems.at[c]
        )
        for c, ref in enumerate(edge_refs)
    ]
    for copy in copies:
        copy.start()
    for copy in copies:
        copy.wait()


def first_edges(in_flight, rows, cols):
    count = in_flight.shape[1] // rows
    return pl.pallas_call(
        edge_kernel,
        in_specs=[pl.BlockSpec(memory_space=pltpu.HBM)],
        out_specs=[VMEM_SPEC] * count,
        out_shape=[pltpu.VMEM((rows, cols), F32)] * count,
        scratch_shapes=[pltpu.SemaphoreType.DMA((count,))],
        compiler_params=pltpu.CompilerParams(vmem_limit_bytes=1 << 20),
        name="first_edges",
        cost_estimate=pl.CostEstimate(
            flops=0, bytes_accessed=8 * count * rows * cols, transcendentals=0
        ),
    )(pltpu.with_memory_space_constraint(in_flight, pltpu.HBM))


def open_kernel(dims, ticks, w_ref, rows_ref, outcome_ref, prior_ref, *rest):
    hi_ref, lo_ref, out_ref, sums_ref, choice_ref, *rest = rest
    stack, buffer, row_buffer, outcome_buffer, prior_buffer, sems = rest
    n_out, local, width, _, _ = dims
    rows = rows_ref.shape[1]
    depth, count = buffer.shape[0], n_out * local
    order = [(n, s) for s in range(local) for n in range(n_out)]
    copies = [
        pltpu.make_async_copy(w_ref.at[n, s], buffer.at[i % depth], sems.at[i % depth])
        for i, (n, s) in enumerate(order)
    ]
    inputs = [
        pltpu.make_async_copy(outcome_ref, outcome_buffer, sems.at[depth]),
        pltpu.make_async_copy(rows_ref, row_buffer, sems.at[depth + 1]),
        pltpu.make_async_copy(prior_ref, prior_buffer, sems.at[depth + 2]),
    ]
    for copy in inputs + copies[:depth]:
        copy.start()
    for copy in inputs:
        copy.wait()
    outcomes = outcome_buffer[:, 0].astype(F32)
    padding = jnp.zeros((LANES - outcomes.shape[0], rows), F32)
    choice_ref[...] = jnp.concatenate([outcomes, padding], axis=0).T
    choice = choice_ref[:, :1]
    for q in range(local):
        put(stack, q, 0, row_buffer[0, :, q * width : (q + 1) * width] * SCALE)
    total = jnp.zeros((rows, LANES), F32)
    selected = None
    for i, (n, s) in enumerate(order):
        copies[i].wait()
        w = buffer[i % depth]
        hi = w.astype(BF)
        lo = (w - hi.astype(F32)).astype(BF)
        hi_ref[n, s] = hi
        lo_ref[n, s] = lo
        if s + n < local:
            value = product(stack[s + n], hi, lo)
            total = total + folded_squares(value)
            selected = jnp.where(choice == n, value, 0.0 if n == 0 else selected)
        if i + depth < count:
            copies[i + depth].start()
        if n == n_out - 1:
            out_ref[:, s * width : (s + 1) * width] = selected
    depth = sums_ref.shape[0]
    row = lax.broadcasted_iota(jnp.int32, (depth, rows), 0)
    prior = jnp.where(lax.axis_index("sector") == 0, jnp.broadcast_to(prior_buffer[...], (depth, rows)), 0.0)
    sums_ref[...] = as_row(1, total, depth) + jnp.where(row == 2 * ticks, prior, 0.0)


def opened(dims, ticks, weights, in_flight, outcomes, prior):
    n_out, local, width, _, _ = dims
    rows = in_flight.shape[1]
    depth = min(BUFFERS, n_out * local)
    operands = [weights, in_flight, outcomes, prior]
    return pl.pallas_call(
        functools.partial(open_kernel, dims, ticks),
        in_specs=[pl.BlockSpec(memory_space=pltpu.HBM)] * len(operands),
        out_specs=[VMEM_SPEC] * 5,
        out_shape=[
            pltpu.VMEM(weights.shape, BF),
            pltpu.VMEM(weights.shape, BF),
            pltpu.VMEM((rows, local * width), F32),
            pltpu.VMEM((sums_depth(ticks), rows), F32),
            pltpu.VMEM((rows, LANES), F32),
        ],
        scratch_shapes=[
            pltpu.VMEM((local, 2 * rows, width), BF),
            pltpu.VMEM((depth, width, width), F32),
            pltpu.VMEM(in_flight.shape, F32),
            pltpu.VMEM(outcomes.shape, jnp.int32),
            pltpu.VMEM(prior.shape, F32),
            pltpu.SemaphoreType.DMA((depth + 3,)),
        ],
        compiler_params=pltpu.CompilerParams(vmem_limit_bytes=2 * VMEM_LIMIT),
        name="opened",
        cost_estimate=pl.CostEstimate(
            flops=3 * rows * n_out * local * width * width,
            bytes_accessed=4 * weights.size,
            transcendentals=0,
        ),
    )(*[pltpu.with_memory_space_constraint(value, pltpu.HBM) for value in operands])


def near_kernel(dims, tick, chunk, *refs):
    choice_ref, hi_ref, lo_ref, main_ref, entering_ref, out_ref, sums_ref, stack = refs
    n_out, local, width, rows, _ = dims
    own = slice(chunk * rows, (chunk + 1) * rows)
    at_start = lax.axis_index("site") == 0
    group = 0
    for q in range(local):
        for start in range(0, width, LANES):
            cols = slice(q * width + start, q * width + start + LANES)
            fresh = entering_ref[tick - 1, own, cols] * SCALE
            value = main_ref[group * rows : (group + 1) * rows]
            put(stack, q, start, jnp.where(at_start, fresh, value))
            group += 1
    choice = choice_ref[own, tick : tick + 1]
    total = jnp.zeros((rows, LANES), F32)
    for s in range(local):
        selected = None
        for n in range(min(n_out, local - s)):
            value = product(stack[s + n], hi_ref[n, s], lo_ref[n, s])
            total = total + folded_squares(value)
            selected = jnp.where(choice == n, value, 0.0 if n == 0 else selected)
        out_ref[:, s * width : (s + 1) * width] = selected
    depth = sums_ref.shape[0]
    old = main_ref[group * rows :, :rows]
    sums_ref[...] = jnp.where(at_start, 0.0, old) + as_row(2 * tick + 1, total, depth)


def far_kernel(dims, tick, ticks, chunk, *refs):
    n_out, local, width, rows, halo = dims
    last = tick == ticks - 1
    refs = list(refs)
    choice_ref, hi_ref, lo_ref, base_ref, base_sums_ref = refs[:5]
    halo_refs = refs[5 : 5 + len(halo)]
    other_refs, stack = refs[5 + len(halo) : -1], refs[-1]
    own = slice(chunk * rows, (chunk + 1) * rows)
    base = slice(None) if base_ref.shape[0] == rows else own
    index = local
    for ref, blocks in zip(halo_refs, halo):
        for q in range(blocks):
            value = ref[:, q * width : (q + 1) * width]
            put(stack, index, 0, value * SCALE if tick == 0 else value)
            index += 1
    if last:
        *done_refs, out_ref, part_ref = other_refs
    else:
        entering_ref, out_ref, edge_ref = other_refs
    at_end = lax.axis_index("site") == lax.axis_size("site") - 1
    choice = choice_ref[own, tick : tick + 1]
    total = jnp.zeros((rows, LANES), F32)
    picked = jnp.zeros((rows, LANES), F32)
    for s in range(local):
        cols = slice(s * width, (s + 1) * width)
        selected = base_ref[base, cols]
        for n in range(max(0, local - s), n_out):
            value = product(stack[s + n], hi_ref[n, s], lo_ref[n, s])
            total = total + folded_squares(value)
            selected = jnp.where(choice == n, value, selected)
        picked = picked + folded_squares(selected)
        if last:
            out_ref[:, cols] = selected
            continue
        for start in range(0, width, LANES):
            at = (s * width + start) // LANES * rows
            out_ref[at : at + rows] = selected[:, start : start + LANES]
        if s < halo[0]:
            fresh = entering_ref[tick, own, cols] * SCALE
            edge_ref[:, cols] = jnp.where(at_end, fresh, selected)
    depth = base_sums_ref.shape[0]
    sums = base_sums_ref[:, base] + as_row(2 * tick + 1, total, depth)
    sums = sums + as_row(2 * tick, picked, depth)
    if last:
        for ref in done_refs:
            part_ref[:, : chunk * rows] = ref[:, : chunk * rows]
        part_ref[:, own] = sums
    else:
        out_ref[local * width // LANES * rows :, :rows] = sums


def step(kernel, dims, blocks, count, outs, operands):
    _, local, width, rows, _ = dims
    return pl.pallas_call(
        kernel,
        in_specs=[VMEM_SPEC] * len(operands),
        out_specs=[VMEM_SPEC] * len(outs),
        out_shape=[pltpu.VMEM(shape, F32) for shape in outs],
        scratch_shapes=[pltpu.VMEM((blocks, 2 * rows, width), BF)],
        compiler_params=pltpu.CompilerParams(vmem_limit_bytes=VMEM_LIMIT),
        cost_estimate=pl.CostEstimate(
            flops=6 * rows * count * width * width,
            bytes_accessed=4 * rows * local * width,
            transcendentals=0,
        ),
    )(*[in_vmem(value) for value in operands])


def near(dims, tick, ticks, chunk, shared, main, entering):
    n_out, local, width, rows, _ = dims
    count = sum(s + n < local for s in range(local) for n in range(n_out))
    outs = [(rows, local * width), (sums_depth(ticks), rows)]
    kernel = functools.partial(near_kernel, dims, tick, chunk)
    operands = [*shared, main, entering]
    return step(kernel, dims, local, count, outs, operands)


def far(dims, tick, ticks, chunk, shared, state, halos, entering, done):
    n_out, local, width, rows, halo = dims
    count = sum(s + n >= local for s in range(local) for n in range(n_out))
    depth = sums_depth(ticks)
    if tick == ticks - 1:
        outs = [(rows, local * width), (depth, CHUNKS * rows)]
        others = done
    else:
        outs = [(local * width // LANES * rows + depth, LANES), (rows, halo[0] * width)]
        others = [entering]
    kernel = functools.partial(far_kernel, dims, tick, ticks, chunk)
    operands = [*shared, *state, *halos, *others]
    blocks = local + sum(halo)
    return step(kernel, dims, blocks, count, outs, operands)


def final_kernel(ticks, bond, chunks, copies, *refs):
    state_refs = refs[:chunks]
    part_refs = refs[chunks : chunks + copies]
    env_ref, logp_ref = refs[chunks + copies :]
    rows = state_refs[0].shape[0]
    sums = [ref[...] for ref in part_refs]
    while len(sums) > 1:
        sums = [sums[i] + sums[i + 1] for i in range(0, len(sums), 2)]
    log_weight = sums[0][2 * ticks : 2 * ticks + 1]
    sums = sums[0] * (1.0 / (bond * SCALE * SCALE))
    factor = jnp.ones_like(log_weight)
    for t in range(ticks):
        picked = sums[2 * t : 2 * t + 1] * factor * factor + EPSILON
        total = sums[2 * t + 1 : 2 * t + 2] * factor * factor + EPSILON
        log_weight = log_weight + jnp.log(picked) - jnp.log(total)
        factor = factor * lax.rsqrt(picked)
    logp_ref[...] = log_weight
    column = jnp.broadcast_to(factor * (1.0 / SCALE), (LANES, factor.shape[1])).T[:, :1]
    for c in range(chunks):
        own = slice(c * rows, (c + 1) * rows)
        env_ref[0, own] = state_refs[c][...] * column[own]


def finish(states, parts, ticks, bond):
    rows = sum(value.shape[0] for value in states)
    span = states[0].shape[1]
    operands = [*states, *parts]
    return pl.pallas_call(
        functools.partial(final_kernel, ticks, float(bond), len(states), len(parts)),
        in_specs=[VMEM_SPEC] * len(operands),
        out_shape=[
            jax.ShapeDtypeStruct((1, rows, span), F32),
            jax.ShapeDtypeStruct((1, rows), F32),
        ],
        compiler_params=pltpu.CompilerParams(vmem_limit_bytes=VMEM_LIMIT),
        name="finish",
    )(*[in_vmem(value) for value in operands])


def sector_terms(value, sectors):
    if sectors & (sectors - 1) or sectors == 1:
        return [lax.psum(value, "sector")]

    def partner(term, mask):
        return lax.ppermute(term, "sector", [(d, d ^ mask) for d in range(sectors)])

    if sectors <= 4:
        return [value] + [partner(value, mask) for mask in range(1, sectors)]
    mask = 1
    while 2 * mask < sectors:
        value = value + partner(value, mask)
        mask *= 2
    return [value, partner(value, mask)]


def per_device(sites, sectors, site_tensor, outcomes, in_flight, prior_logp, entering):
    weights = site_tensor[0]
    n_out, local, width = weights.shape[:3]
    span = in_flight.shape[2]
    ticks = outcomes.shape[0]
    rows = in_flight.shape[1] // CHUNKS
    need = n_out - 1
    halo = []
    while need > 0:
        halo.append(min(local, need))
        need -= halo[-1]
    dims = (n_out, local, width, rows, tuple(halo))
    up = [(k, k + 1) for k in range(sites - 1)]

    def moved(edge, shift):
        pieces = []
        for hop, blocks in enumerate(halo):
            pairs = [
                (k * sectors + d + hop + 1, (k + shift) % sites * sectors + d)
                for k in range(sites)
                for d in range(sectors - hop - 1)
            ]
            pieces.append(lax.ppermute(edge[:, : blocks * width], ("site", "sector"), pairs))
        return pieces

    edges = first_edges(in_flight, rows, halo[0] * width)
    halos = [moved(edges[c], 0) for c in range(CHUNKS)]
    hi, lo, base, base_sums, choice = opened(
        dims, ticks, weights, in_flight, outcomes, prior_logp
    )
    shared = [choice, hi, lo]
    states = [(base, base_sums)] * CHUNKS
    mains = [None] * CHUNKS
    done = []
    for tick in range(ticks):
        for c in range(CHUNKS):
            if tick > 0:
                states[c] = near(dims, tick, ticks, c, shared, mains[c], entering)
            mains[c], other = far(
                dims, tick, ticks, c, shared, states[c], halos[c], entering, done
            )
            if tick == ticks - 1:
                done = [other]
                continue
            mains[c] = lax.ppermute(mains[c], "site", up)
            halos[c] = moved(other, 1)
    parts = sector_terms(done[0], sectors)
    return tuple(finish(mains, parts, ticks, span * sectors))


def solution(mesh):
    sizes = (mesh.shape["site"], mesh.shape["sector"])

    def whole(site_tensor, outcomes, *others):
        call = jax.shard_map(
            functools.partial(per_device, *sizes),
            mesh=mesh,
            in_specs=(
                P("site", None, "sector", None, None),
                P(None, "site", None),
                P("site", None, "sector"),
                P("site", None),
                P(None, None, "sector"),
            ),
            out_specs=(P("site", None, "sector"), P("site", None)),
            check_vma=False,
        )
        return call(site_tensor, outcomes, *others)

    return whole
```

```python
import functools

import jax
import jax.numpy as jnp
from jax import lax
from jax.experimental import pallas as pl
from jax.experimental.pallas import tpu as pltpu
from jax.sharding import PartitionSpec as P


EPSILON = 1e-06
SCALE = 256.0
LANES = 128
CHUNKS = 2
BUFFERS = 8
VMEM_LIMIT = 12 << 20
BF = jnp.bfloat16
F32 = jnp.float32
VMEM_SPEC = pl.BlockSpec(memory_space=pltpu.VMEM)


def sums_depth(ticks):
    return -(-(2 * ticks + 1) // 8) * 8


def in_vmem(value):
    return pltpu.with_memory_space_constraint(value, pltpu.VMEM)


def put(stack, index, start, value):
    rows, cols = value.shape
    hi = value.astype(BF)
    stack[index, :rows, start : start + cols] = hi
    stack[index, rows:, start : start + cols] = (value - hi.astype(F32)).astype(BF)


def product(both, hi, lo):
    rows = both.shape[0] // 2
    wide = jnp.dot(both, hi, preferred_element_type=F32)
    value = wide[:rows] + wide[rows:]
    return value + jnp.dot(both[:rows], lo, preferred_element_type=F32)


def folded_squares(value):
    square = value * value
    total = square[:, :LANES]
    for start in range(LANES, square.shape[1], LANES):
        total = total + square[:, start : start + LANES]
    return total


def as_row(index, squares, depth):
    rows = squares.shape[0]
    lane = lax.broadcasted_iota(jnp.int32, (rows, LANES), 1)
    column = jnp.sum(squares, axis=1, keepdims=True)
    return jnp.where(lane == index, column, 0.0).T[:depth]


def edge_kernel(rows_ref, *rest):
    *edge_refs, sems = rest
    rows, cols = edge_refs[0].shape
    copies = [
        pltpu.make_async_copy(
            rows_ref.at[0, pl.ds(c * rows, rows), pl.ds(0, cols)], ref, sems.at[c]
        )
        for c, ref in enumerate(edge_refs)
    ]
    for copy in copies:
        copy.start()
    for copy in copies:
        copy.wait()


def first_edges(in_flight, rows, cols):
    count = in_flight.shape[1] // rows
    return pl.pallas_call(
        edge_kernel,
        in_specs=[pl.BlockSpec(memory_space=pltpu.HBM)],
        out_specs=[VMEM_SPEC] * count,
        out_shape=[pltpu.VMEM((rows, cols), F32)] * count,
        scratch_shapes=[pltpu.SemaphoreType.DMA((count,))],
        compiler_params=pltpu.CompilerParams(vmem_limit_bytes=1 << 20),
        name="first_edges",
        cost_estimate=pl.CostEstimate(
            flops=0, bytes_accessed=8 * count * rows * cols, transcendentals=0
        ),
    )(pltpu.with_memory_space_constraint(in_flight, pltpu.HBM))


def open_kernel(dims, ticks, w_ref, rows_ref, outcome_ref, prior_ref, *rest):
    hi_ref, lo_ref, out_ref, sums_ref, choice_ref, *rest = rest
    stack, buffer, row_buffer, outcome_buffer, prior_buffer, sems = rest
    n_out, local, width, _, _ = dims
    rows = rows_ref.shape[1]
    depth, count = buffer.shape[0], n_out * local
    order = [(n, s) for s in range(local) for n in range(n_out) if s + n >= local]
    alone = len(order)
    order += [(n, s) for s in range(local) for n in range(n_out) if s + n < local]
    copies = [
        pltpu.make_async_copy(w_ref.at[n, s], buffer.at[i % depth], sems.at[i % depth])
        for i, (n, s) in enumerate(order)
    ]
    inputs = [
        pltpu.make_async_copy(outcome_ref, outcome_buffer, sems.at[depth]),
        pltpu.make_async_copy(rows_ref, row_buffer, sems.at[depth + 1]),
        pltpu.make_async_copy(prior_ref, prior_buffer, sems.at[depth + 2]),
    ]
    for copy in inputs + copies[:depth]:
        copy.start()

    def split(i):
        n, s = order[i]
        copies[i].wait()
        w = buffer[i % depth]
        hi = w.astype(BF)
        lo = (w - hi.astype(F32)).astype(BF)
        hi_ref[n, s] = hi
        lo_ref[n, s] = lo
        if i + depth < count:
            copies[i + depth].start()
        return hi, lo

    for i in range(alone):
        split(i)
    for copy in inputs:
        copy.wait()
    outcomes = outcome_buffer[:, 0].astype(F32)
    padding = jnp.zeros((LANES - outcomes.shape[0], rows), F32)
    choice_ref[...] = jnp.concatenate([outcomes, padding], axis=0).T
    choice = choice_ref[:, :1]
    for q in range(local):
        put(stack, q, 0, row_buffer[0, :, q * width : (q + 1) * width] * SCALE)
    total = jnp.zeros((rows, LANES), F32)
    selected = None
    for i in range(alone, count):
        n, s = order[i]
        value = product(stack[s + n], *split(i))
        total = total + folded_squares(value)
        selected = jnp.where(choice == n, value, 0.0 if n == 0 else selected)
        if n == min(n_out, local - s) - 1:
            out_ref[:, s * width : (s + 1) * width] = selected
    depth = sums_ref.shape[0]
    row = lax.broadcasted_iota(jnp.int32, (depth, rows), 0)
    prior = jnp.where(lax.axis_index("sector") == 0, jnp.broadcast_to(prior_buffer[...], (depth, rows)), 0.0)
    sums_ref[...] = as_row(1, total, depth) + jnp.where(row == 2 * ticks, prior, 0.0)


def opened(dims, ticks, weights, in_flight, outcomes, prior):
    n_out, local, width, _, _ = dims
    rows = in_flight.shape[1]
    depth = min(BUFFERS, n_out * local)
    operands = [weights, in_flight, outcomes, prior]
    return pl.pallas_call(
        functools.partial(open_kernel, dims, ticks),
        in_specs=[pl.BlockSpec(memory_space=pltpu.HBM)] * len(operands),
        out_specs=[VMEM_SPEC] * 5,
        out_shape=[
            pltpu.VMEM(weights.shape, BF),
            pltpu.VMEM(weights.shape, BF),
            pltpu.VMEM((rows, local * width), F32),
            pltpu.VMEM((sums_depth(ticks), rows), F32),
            pltpu.VMEM((rows, LANES), F32),
        ],
        scratch_shapes=[
            pltpu.VMEM((local, 2 * rows, width), BF),
            pltpu.VMEM((depth, width, width), F32),
            pltpu.VMEM(in_flight.shape, F32),
            pltpu.VMEM(outcomes.shape, jnp.int32),
            pltpu.VMEM(prior.shape, F32),
            pltpu.SemaphoreType.DMA((depth + 3,)),
        ],
        compiler_params=pltpu.CompilerParams(vmem_limit_bytes=2 * VMEM_LIMIT),
        name="opened",
        cost_estimate=pl.CostEstimate(
            flops=3 * rows * n_out * local * width * width,
            bytes_accessed=4 * weights.size,
            transcendentals=0,
        ),
    )(*[pltpu.with_memory_space_constraint(value, pltpu.HBM) for value in operands])


def near_kernel(dims, tick, chunk, *refs):
    choice_ref, hi_ref, lo_ref, main_ref, entering_ref, *refs = refs
    out_ref, sums_ref, stack, fresh, sem = refs
    n_out, local, width, rows, _ = dims
    own = slice(chunk * rows, (chunk + 1) * rows)
    at_start = lax.axis_index("site") == 0
    groups = local * width // LANES

    @pl.when(at_start)
    def _():
        source = entering_ref.at[tick - 1, pl.ds(own.start, rows), :]
        copy = pltpu.make_async_copy(source, fresh, sem)
        copy.start()
        copy.wait()
        for q in range(local):
            put(stack, q, 0, fresh[:, q * width : (q + 1) * width] * SCALE)

    @pl.when(jnp.logical_not(at_start))
    def _():
        for group in range(groups):
            q, start = divmod(group * LANES, width)
            put(stack, q, start, main_ref[group * rows : (group + 1) * rows])

    choice = choice_ref[own, tick : tick + 1]
    total = jnp.zeros((rows, LANES), F32)
    for s in range(local):
        selected = None
        for n in range(min(n_out, local - s)):
            value = product(stack[s + n], hi_ref[n, s], lo_ref[n, s])
            total = total + folded_squares(value)
            selected = jnp.where(choice == n, value, 0.0 if n == 0 else selected)
        out_ref[:, s * width : (s + 1) * width] = selected
    depth = sums_ref.shape[0]
    old = main_ref[groups * rows :, :rows]
    sums_ref[...] = jnp.where(at_start, 0.0, old) + as_row(2 * tick + 1, total, depth)


def far_kernel(dims, tick, ticks, chunk, *refs):
    n_out, local, width, rows, halo = dims
    last = tick == ticks - 1
    refs = list(refs)
    choice_ref, hi_ref, lo_ref, base_ref, base_sums_ref = refs[:5]
    halo_refs, other_refs = refs[5 : 5 + len(halo)], refs[5 + len(halo) :]
    if last:
        *done_refs, out_ref, part_ref, stack = other_refs
    else:
        entering_ref, out_ref, edge_ref, stack, fresh, sem = other_refs
    own = slice(chunk * rows, (chunk + 1) * rows)
    base = slice(None) if base_ref.shape[0] == rows else own
    index = local
    for ref, blocks in zip(halo_refs, halo):
        for q in range(blocks):
            value = ref[:, q * width : (q + 1) * width]
            put(stack, index, 0, value * SCALE if tick == 0 else value)
            index += 1
    at_end = lax.axis_index("site") == lax.axis_size("site") - 1
    if not last:
        cols = edge_ref.shape[1]
        source = entering_ref.at[tick, pl.ds(own.start, rows), pl.ds(0, cols)]
        copy = pltpu.make_async_copy(source, fresh, sem)
        pl.when(at_end)(copy.start)
    choice = choice_ref[own, tick : tick + 1]
    total = jnp.zeros((rows, LANES), F32)
    picked = jnp.zeros((rows, LANES), F32)
    for s in range(local):
        cols = slice(s * width, (s + 1) * width)
        selected = base_ref[base, cols]
        for n in range(max(0, local - s), n_out):
            value = product(stack[s + n], hi_ref[n, s], lo_ref[n, s])
            total = total + folded_squares(value)
            selected = jnp.where(choice == n, value, selected)
        picked = picked + folded_squares(selected)
        if last:
            out_ref[:, cols] = selected
            continue
        for start in range(0, width, LANES):
            at = (s * width + start) // LANES * rows
            out_ref[at : at + rows] = selected[:, start : start + LANES]
        if s < halo[0]:
            edge_ref[:, cols] = selected
    if not last:

        @pl.when(at_end)
        def _():
            copy.wait()
            edge_ref[...] = fresh[...] * SCALE

    depth = base_sums_ref.shape[0]
    sums = base_sums_ref[:, base] + as_row(2 * tick + 1, total, depth)
    sums = sums + as_row(2 * tick, picked, depth)
    if last:
        for ref in done_refs:
            part_ref[:, : chunk * rows] = ref[:, : chunk * rows]
        part_ref[:, own] = sums
    else:
        out_ref[local * width // LANES * rows :, :rows] = sums


def step(kernel, dims, blocks, count, outs, operands, entering=None, cols=0):
    _, local, width, rows, _ = dims
    specs = [VMEM_SPEC] * len(operands)
    operands = [in_vmem(value) for value in operands]
    scratch = [pltpu.VMEM((blocks, 2 * rows, width), BF)]
    if entering is not None:
        specs.append(pl.BlockSpec(memory_space=pltpu.HBM))
        operands.append(pltpu.with_memory_space_constraint(entering, pltpu.HBM))
        scratch += [pltpu.VMEM((rows, cols), F32), pltpu.SemaphoreType.DMA]
    return pl.pallas_call(
        kernel,
        in_specs=specs,
        out_specs=[VMEM_SPEC] * len(outs),
        out_shape=[pltpu.VMEM(shape, F32) for shape in outs],
        scratch_shapes=scratch,
        compiler_params=pltpu.CompilerParams(vmem_limit_bytes=VMEM_LIMIT),
        cost_estimate=pl.CostEstimate(
            flops=6 * rows * count * width * width,
            bytes_accessed=4 * rows * local * width,
            transcendentals=0,
        ),
    )(*operands)


def near(dims, tick, ticks, chunk, shared, main, entering):
    n_out, local, width, rows, _ = dims
    count = sum(s + n < local for s in range(local) for n in range(n_out))
    outs = [(rows, local * width), (sums_depth(ticks), rows)]
    kernel = functools.partial(near_kernel, dims, tick, chunk)
    operands = [*shared, main]
    return step(kernel, dims, local, count, outs, operands, entering, local * width)


def far(dims, tick, ticks, chunk, shared, state, halos, entering, done):
    n_out, local, width, rows, halo = dims
    count = sum(s + n >= local for s in range(local) for n in range(n_out))
    depth = sums_depth(ticks)
    if tick == ticks - 1:
        outs = [(rows, local * width), (depth, CHUNKS * rows)]
        operands, fresh = [*shared, *state, *halos, *done], None
    else:
        outs = [(local * width // LANES * rows + depth, LANES), (rows, halo[0] * width)]
        operands, fresh = [*shared, *state, *halos], entering
    kernel = functools.partial(far_kernel, dims, tick, ticks, chunk)
    blocks = local + sum(halo)
    return step(kernel, dims, blocks, count, outs, operands, fresh, halo[0] * width)


def final_kernel(ticks, bond, chunks, copies, *refs):
    state_refs = refs[:chunks]
    part_refs = refs[chunks : chunks + copies]
    env_ref, logp_ref = refs[chunks + copies :]
    rows = state_refs[0].shape[0]
    sums = [ref[...] for ref in part_refs]
    while len(sums) > 1:
        sums = [sums[i] + sums[i + 1] for i in range(0, len(sums), 2)]
    log_weight = sums[0][2 * ticks : 2 * ticks + 1]
    sums = sums[0] * (1.0 / (bond * SCALE * SCALE))
    factor = jnp.ones_like(log_weight)
    for t in range(ticks):
        picked = sums[2 * t : 2 * t + 1] * factor * factor + EPSILON
        total = sums[2 * t + 1 : 2 * t + 2] * factor * factor + EPSILON
        log_weight = log_weight + jnp.log(picked) - jnp.log(total)
        factor = factor * lax.rsqrt(picked)
    logp_ref[...] = log_weight
    column = jnp.broadcast_to(factor * (1.0 / SCALE), (LANES, factor.shape[1])).T[:, :1]
    for c in range(chunks):
        own = slice(c * rows, (c + 1) * rows)
        env_ref[0, own] = state_refs[c][...] * column[own]


def finish(states, parts, ticks, bond):
    rows = sum(value.shape[0] for value in states)
    span = states[0].shape[1]
    operands = [*states, *parts]
    return pl.pallas_call(
        functools.partial(final_kernel, ticks, float(bond), len(states), len(parts)),
        in_specs=[VMEM_SPEC] * len(operands),
        out_shape=[
            jax.ShapeDtypeStruct((1, rows, span), F32),
            jax.ShapeDtypeStruct((1, rows), F32),
        ],
        compiler_params=pltpu.CompilerParams(vmem_limit_bytes=VMEM_LIMIT),
        name="finish",
    )(*[in_vmem(value) for value in operands])


def sector_terms(value, sectors):
    if sectors & (sectors - 1) or sectors == 1:
        return [lax.psum(value, "sector")]

    def partner(term, mask):
        return lax.ppermute(term, "sector", [(d, d ^ mask) for d in range(sectors)])

    if sectors <= 4:
        return [value] + [partner(value, mask) for mask in range(1, sectors)]
    mask = 1
    while 2 * mask < sectors:
        value = value + partner(value, mask)
        mask *= 2
    return [value, partner(value, mask)]


def per_device(sites, sectors, site_tensor, outcomes, in_flight, prior_logp, entering):
    weights = site_tensor[0]
    n_out, local, width = weights.shape[:3]
    span = in_flight.shape[2]
    ticks = outcomes.shape[0]
    rows = in_flight.shape[1] // CHUNKS
    need = n_out - 1
    halo = []
    while need > 0:
        halo.append(min(local, need))
        need -= halo[-1]
    dims = (n_out, local, width, rows, tuple(halo))
    up = [(k, k + 1) for k in range(sites - 1)]

    def moved(edge, shift):
        pieces = []
        for hop, blocks in enumerate(halo):
            pairs = [
                (k * sectors + d + hop + 1, (k + shift) % sites * sectors + d)
                for k in range(sites)
                for d in range(sectors - hop - 1)
            ]
            pieces.append(lax.ppermute(edge[:, : blocks * width], ("site", "sector"), pairs))
        return pieces

    edges = first_edges(in_flight, rows, halo[0] * width)
    halos = [moved(edges[c], 0) for c in range(CHUNKS)]
    hi, lo, base, base_sums, choice = opened(dims, ticks, weights, in_flight, outcomes, prior_logp)
    shared = [choice, hi, lo]
    states = [(base, base_sums)] * CHUNKS
    mains = [None] * CHUNKS
    done = []
    for tick in range(ticks):
        for c in range(CHUNKS):
            if tick > 0:
                states[c] = near(dims, tick, ticks, c, shared, mains[c], entering)
            mains[c], other = far(dims, tick, ticks, c, shared, states[c], halos[c], entering, done)
            if tick == ticks - 1:
                done = [other]
                continue
            mains[c] = lax.ppermute(mains[c], "site", up)
            halos[c] = moved(other, 1)
    parts = sector_terms(done[0], sectors)
    return tuple(finish(mains, parts, ticks, span * sectors))


def solution(mesh):
    sizes = (mesh.shape["site"], mesh.shape["sector"])

    def whole(site_tensor, outcomes, *others):
        call = jax.shard_map(
            functools.partial(per_device, *sizes),
            mesh=mesh,
            in_specs=(
                P("site", None, "sector", None, None),
                P(None, "site", None),
                P("site", None, "sector"),
                P("site", None),
                P(None, None, "sector"),
            ),
            out_specs=(P("site", None, "sector"), P("site", None)),
            check_vma=False,
        )
        return call(site_tensor, outcomes, *others)

    return whole
```

```python
import functools

import jax
import jax.numpy as jnp
from jax import lax
from jax.experimental import pallas as pl
from jax.experimental.pallas import tpu as pltpu
from jax.sharding import PartitionSpec as P


EPSILON = 1e-06
SCALE = 256.0
LANES = 128
CHUNKS = 2
BUFFERS = 8
VMEM_LIMIT = 12 << 20
BF = jnp.bfloat16
F32 = jnp.float32
VMEM_SPEC = pl.BlockSpec(memory_space=pltpu.VMEM)


def sums_depth(ticks):
    return -(-(2 * ticks + 1) // 8) * 8


def in_vmem(value):
    return pltpu.with_memory_space_constraint(value, pltpu.VMEM)


def put(stack, index, start, value):
    rows, cols = value.shape
    hi = value.astype(BF)
    stack[index, :rows, start : start + cols] = hi
    stack[index, rows:, start : start + cols] = (value - hi.astype(F32)).astype(BF)


def product(both, hi, lo):
    rows = both.shape[0] // 2
    wide = jnp.dot(both, hi, preferred_element_type=F32)
    value = wide[:rows] + wide[rows:]
    return value + jnp.dot(both[:rows], lo, preferred_element_type=F32)


def folded_squares(value):
    square = value * value
    total = square[:, :LANES]
    for start in range(LANES, square.shape[1], LANES):
        total = total + square[:, start : start + LANES]
    return total


def as_row(index, squares, depth):
    rows = squares.shape[0]
    lane = lax.broadcasted_iota(jnp.int32, (rows, LANES), 1)
    column = jnp.sum(squares, axis=1, keepdims=True)
    return jnp.where(lane == index, column, 0.0).T[:depth]


def edge_kernel(rows_ref, *rest):
    *edge_refs, sems = rest
    rows, cols = edge_refs[0].shape
    copies = [
        pltpu.make_async_copy(
            rows_ref.at[0, pl.ds(c * rows, rows), pl.ds(0, cols)], ref, sems.at[c]
        )
        for c, ref in enumerate(edge_refs)
    ]
    for copy in copies:
        copy.start()
    for copy in copies:
        copy.wait()


def first_edges(in_flight, rows, cols):
    count = in_flight.shape[1] // rows
    return pl.pallas_call(
        edge_kernel,
        in_specs=[pl.BlockSpec(memory_space=pltpu.HBM)],
        out_specs=[VMEM_SPEC] * count,
        out_shape=[pltpu.VMEM((rows, cols), F32)] * count,
        scratch_shapes=[pltpu.SemaphoreType.DMA((count,))],
        compiler_params=pltpu.CompilerParams(vmem_limit_bytes=1 << 20),
        name="first_edges",
        cost_estimate=pl.CostEstimate(
            flops=0, bytes_accessed=8 * count * rows * cols, transcendentals=0
        ),
    )(pltpu.with_memory_space_constraint(in_flight, pltpu.HBM))


def open_kernel(dims, ticks, w_ref, rows_ref, outcome_ref, prior_ref, *rest):
    hi_ref, lo_ref, out_ref, sums_ref, choice_ref, *rest = rest
    stack, buffer, row_buffer, outcome_buffer, prior_buffer, sems = rest
    n_out, local, width, _, _ = dims
    rows = rows_ref.shape[1]
    depth, count = buffer.shape[0], n_out * local
    order = [(n, s) for s in range(local) for n in range(n_out) if s + n >= local]
    alone = len(order)
    order += [(n, s) for s in range(local) for n in range(n_out) if s + n < local]
    copies = [
        pltpu.make_async_copy(w_ref.at[n, s], buffer.at[i % depth], sems.at[i % depth])
        for i, (n, s) in enumerate(order)
    ]
    inputs = [
        pltpu.make_async_copy(outcome_ref, outcome_buffer, sems.at[depth]),
        pltpu.make_async_copy(rows_ref, row_buffer, sems.at[depth + 1]),
        pltpu.make_async_copy(prior_ref, prior_buffer, sems.at[depth + 2]),
    ]
    for copy in copies[:depth] + inputs:
        copy.start()

    def split(i):
        n, s = order[i]
        copies[i].wait()
        w = buffer[i % depth]
        hi = w.astype(BF)
        lo = (w - hi.astype(F32)).astype(BF)
        hi_ref[n, s] = hi
        lo_ref[n, s] = lo
        if i + depth < count:
            copies[i + depth].start()
        return hi, lo

    for i in range(alone):
        split(i)
    for copy in inputs:
        copy.wait()
    outcomes = outcome_buffer[:, 0].astype(F32)
    padding = jnp.zeros((LANES - outcomes.shape[0], rows), F32)
    choice_ref[...] = jnp.concatenate([outcomes, padding], axis=0).T
    choice = choice_ref[:, :1]
    for q in range(local):
        put(stack, q, 0, row_buffer[0, :, q * width : (q + 1) * width] * SCALE)
    total = jnp.zeros((rows, LANES), F32)
    selected = None
    for i in range(alone, count):
        n, s = order[i]
        value = product(stack[s + n], *split(i))
        total = total + folded_squares(value)
        selected = jnp.where(choice == n, value, 0.0 if n == 0 else selected)
        if n == min(n_out, local - s) - 1:
            out_ref[:, s * width : (s + 1) * width] = selected
    depth = sums_ref.shape[0]
    row = lax.broadcasted_iota(jnp.int32, (depth, rows), 0)
    prior = jnp.where(lax.axis_index("sector") == 0, jnp.broadcast_to(prior_buffer[...], (depth, rows)), 0.0)
    sums_ref[...] = as_row(1, total, depth) + jnp.where(row == 2 * ticks, prior, 0.0)


def opened(dims, ticks, weights, in_flight, outcomes, prior):
    n_out, local, width, _, _ = dims
    rows = in_flight.shape[1]
    depth = min(BUFFERS, n_out * local)
    operands = [weights, in_flight, outcomes, prior]
    return pl.pallas_call(
        functools.partial(open_kernel, dims, ticks),
        in_specs=[pl.BlockSpec(memory_space=pltpu.HBM)] * len(operands),
        out_specs=[VMEM_SPEC] * 5,
        out_shape=[
            pltpu.VMEM(weights.shape, BF),
            pltpu.VMEM(weights.shape, BF),
            pltpu.VMEM((rows, local * width), F32),
            pltpu.VMEM((sums_depth(ticks), rows), F32),
            pltpu.VMEM((rows, LANES), F32),
        ],
        scratch_shapes=[
            pltpu.VMEM((local, 2 * rows, width), BF),
            pltpu.VMEM((depth, width, width), F32),
            pltpu.VMEM(in_flight.shape, F32),
            pltpu.VMEM(outcomes.shape, jnp.int32),
            pltpu.VMEM(prior.shape, F32),
            pltpu.SemaphoreType.DMA((depth + 3,)),
        ],
        compiler_params=pltpu.CompilerParams(vmem_limit_bytes=2 * VMEM_LIMIT),
        name="opened",
        cost_estimate=pl.CostEstimate(
            flops=3 * rows * n_out * local * width * width,
            bytes_accessed=4 * weights.size,
            transcendentals=0,
        ),
    )(*[pltpu.with_memory_space_constraint(value, pltpu.HBM) for value in operands])


def near_kernel(dims, tick, chunk, *refs):
    choice_ref, hi_ref, lo_ref, main_ref, entering_ref, *refs = refs
    out_ref, sums_ref, stack, fresh, sem = refs
    n_out, local, width, rows, _ = dims
    own = slice(chunk * rows, (chunk + 1) * rows)
    at_start = lax.axis_index("site") == 0
    groups = local * width // LANES

    @pl.when(at_start)
    def _():
        source = entering_ref.at[tick - 1, pl.ds(own.start, rows), :]
        copy = pltpu.make_async_copy(source, fresh, sem)
        copy.start()
        copy.wait()

        @pl.loop(0, local)
        def _(q):
            cols = pl.ds(pl.multiple_of(q * width, LANES), width)
            put(stack, q, 0, fresh[:, cols] * SCALE)

    @pl.when(jnp.logical_not(at_start))
    def _():
        for group in range(groups):
            q, start = divmod(group * LANES, width)
            put(stack, q, start, main_ref[group * rows : (group + 1) * rows])

    choice = choice_ref[own, tick : tick + 1]
    total = jnp.zeros((rows, LANES), F32)
    for s in range(local):
        selected = None
        for n in range(min(n_out, local - s)):
            value = product(stack[s + n], hi_ref[n, s], lo_ref[n, s])
            total = total + folded_squares(value)
            selected = jnp.where(choice == n, value, 0.0 if n == 0 else selected)
        out_ref[:, s * width : (s + 1) * width] = selected
    depth = sums_ref.shape[0]
    old = main_ref[groups * rows :, :rows]
    sums_ref[...] = jnp.where(at_start, 0.0, old) + as_row(2 * tick + 1, total, depth)


def far_kernel(dims, tick, ticks, chunk, *refs):
    n_out, local, width, rows, halo = dims
    last = tick == ticks - 1
    refs = list(refs)
    choice_ref, hi_ref, lo_ref, base_ref, base_sums_ref = refs[:5]
    halo_refs, other_refs = refs[5 : 5 + len(halo)], refs[5 + len(halo) :]
    if last:
        *done_refs, out_ref, part_ref, stack = other_refs
    else:
        entering_ref, out_ref, edge_ref, stack, fresh, sem = other_refs
    own = slice(chunk * rows, (chunk + 1) * rows)
    base = slice(None) if base_ref.shape[0] == rows else own
    index = local
    for ref, blocks in zip(halo_refs, halo):
        for q in range(blocks):
            value = ref[:, q * width : (q + 1) * width]
            put(stack, index, 0, value * SCALE if tick == 0 else value)
            index += 1
    at_end = lax.axis_index("site") == lax.axis_size("site") - 1
    if not last:
        cols_sent = edge_ref.shape[1]
        source = entering_ref.at[tick, pl.ds(own.start, rows), pl.ds(0, cols_sent)]
        copy = pltpu.make_async_copy(source, fresh, sem)
        pl.when(at_end)(copy.start)
    choice = choice_ref[own, tick : tick + 1]
    total = jnp.zeros((rows, LANES), F32)
    picked = jnp.zeros((rows, LANES), F32)
    for s in range(local):
        cols = slice(s * width, (s + 1) * width)
        selected = base_ref[base, cols]
        for n in range(max(0, local - s), n_out):
            value = product(stack[s + n], hi_ref[n, s], lo_ref[n, s])
            total = total + folded_squares(value)
            selected = jnp.where(choice == n, value, selected)
        picked = picked + folded_squares(selected)
        if last:
            out_ref[:, cols] = selected
            continue
        for start in range(0, width, LANES):
            at = (s * width + start) // LANES * rows
            out_ref[at : at + rows] = selected[:, start : start + LANES]
        if s < halo[0]:
            edge_ref[:, cols] = selected
    if not last:

        @pl.when(at_end)
        def _():
            copy.wait()

            @pl.loop(0, cols_sent // LANES)
            def _(group):
                cols = pl.ds(pl.multiple_of(group * LANES, LANES), LANES)
                edge_ref[:, cols] = fresh[:, cols] * SCALE

    depth = base_sums_ref.shape[0]
    sums = base_sums_ref[:, base] + as_row(2 * tick + 1, total, depth)
    sums = sums + as_row(2 * tick, picked, depth)
    if last:
        for ref in done_refs:
            part_ref[:, : chunk * rows] = ref[:, : chunk * rows]
        part_ref[:, own] = sums
    else:
        out_ref[local * width // LANES * rows :, :rows] = sums


def step(kernel, dims, blocks, count, outs, operands, entering=None, cols=0):
    _, local, width, rows, _ = dims
    specs = [VMEM_SPEC] * len(operands)
    operands = [in_vmem(value) for value in operands]
    scratch = [pltpu.VMEM((blocks, 2 * rows, width), BF)]
    if entering is not None:
        specs.append(pl.BlockSpec(memory_space=pltpu.HBM))
        operands.append(pltpu.with_memory_space_constraint(entering, pltpu.HBM))
        scratch += [pltpu.VMEM((rows, cols), F32), pltpu.SemaphoreType.DMA]
    return pl.pallas_call(
        kernel,
        in_specs=specs,
        out_specs=[VMEM_SPEC] * len(outs),
        out_shape=[pltpu.VMEM(shape, F32) for shape in outs],
        scratch_shapes=scratch,
        compiler_params=pltpu.CompilerParams(vmem_limit_bytes=VMEM_LIMIT),
        cost_estimate=pl.CostEstimate(
            flops=6 * rows * count * width * width,
            bytes_accessed=4 * rows * local * width,
            transcendentals=0,
        ),
    )(*operands)


def near(dims, tick, ticks, chunk, shared, main, entering):
    n_out, local, width, rows, _ = dims
    count = sum(s + n < local for s in range(local) for n in range(n_out))
    outs = [(rows, local * width), (sums_depth(ticks), rows)]
    kernel = functools.partial(near_kernel, dims, tick, chunk)
    operands = [*shared, main]
    return step(kernel, dims, local, count, outs, operands, entering, local * width)


def far(dims, tick, ticks, chunk, shared, state, halos, entering, done):
    n_out, local, width, rows, halo = dims
    count = sum(s + n >= local for s in range(local) for n in range(n_out))
    depth = sums_depth(ticks)
    if tick == ticks - 1:
        outs = [(rows, local * width), (depth, CHUNKS * rows)]
        operands, fresh = [*shared, *state, *halos, *done], None
    else:
        outs = [(local * width // LANES * rows + depth, LANES), (rows, halo[0] * width)]
        operands, fresh = [*shared, *state, *halos], entering
    kernel = functools.partial(far_kernel, dims, tick, ticks, chunk)
    blocks = local + sum(halo)
    return step(kernel, dims, blocks, count, outs, operands, fresh, halo[0] * width)


def final_kernel(ticks, bond, chunks, copies, *refs):
    state_refs = refs[:chunks]
    part_refs = refs[chunks : chunks + copies]
    env_ref, logp_ref = refs[chunks + copies :]
    rows = state_refs[0].shape[0]
    sums = [ref[...] for ref in part_refs]
    while len(sums) > 1:
        sums = [sums[i] + sums[i + 1] for i in range(0, len(sums), 2)]
    log_weight = sums[0][2 * ticks : 2 * ticks + 1]
    sums = sums[0] * (1.0 / (bond * SCALE * SCALE))
    factor = jnp.ones_like(log_weight)
    for t in range(ticks):
        picked = sums[2 * t : 2 * t + 1] * factor * factor + EPSILON
        total = sums[2 * t + 1 : 2 * t + 2] * factor * factor + EPSILON
        log_weight = log_weight + jnp.log(picked) - jnp.log(total)
        factor = factor * lax.rsqrt(picked)
    logp_ref[...] = log_weight
    column = jnp.broadcast_to(factor * (1.0 / SCALE), (LANES, factor.shape[1])).T[:, :1]
    for c in range(chunks):
        own = slice(c * rows, (c + 1) * rows)
        env_ref[0, own] = state_refs[c][...] * column[own]


def finish(states, parts, ticks, bond):
    rows = sum(value.shape[0] for value in states)
    span = states[0].shape[1]
    operands = [*states, *parts]
    return pl.pallas_call(
        functools.partial(final_kernel, ticks, float(bond), len(states), len(parts)),
        in_specs=[VMEM_SPEC] * len(operands),
        out_shape=[
            jax.ShapeDtypeStruct((1, rows, span), F32),
            jax.ShapeDtypeStruct((1, rows), F32),
        ],
        compiler_params=pltpu.CompilerParams(vmem_limit_bytes=VMEM_LIMIT),
        name="finish",
    )(*[in_vmem(value) for value in operands])


def sector_terms(value, sectors):
    if sectors & (sectors - 1) or sectors == 1:
        return [lax.psum(value, "sector")]

    def partner(term, mask):
        return lax.ppermute(term, "sector", [(d, d ^ mask) for d in range(sectors)])

    if sectors <= 4:
        return [value] + [partner(value, mask) for mask in range(1, sectors)]
    mask = 1
    while 2 * mask < sectors:
        value = value + partner(value, mask)
        mask *= 2
    return [value, partner(value, mask)]


def per_device(sites, sectors, site_tensor, outcomes, in_flight, prior_logp, entering):
    weights = site_tensor[0]
    n_out, local, width = weights.shape[:3]
    span = in_flight.shape[2]
    ticks = outcomes.shape[0]
    rows = in_flight.shape[1] // CHUNKS
    need = n_out - 1
    halo = []
    while need > 0:
        halo.append(min(local, need))
        need -= halo[-1]
    dims = (n_out, local, width, rows, tuple(halo))
    up = [(k, k + 1) for k in range(sites - 1)]

    def moved(edge, shift):
        pieces = []
        for hop, blocks in enumerate(halo):
            pairs = [
                (k * sectors + d + hop + 1, (k + shift) % sites * sectors + d)
                for k in range(sites)
                for d in range(sectors - hop - 1)
            ]
            pieces.append(lax.ppermute(edge[:, : blocks * width], ("site", "sector"), pairs))
        return pieces

    edges = first_edges(in_flight, rows, halo[0] * width)
    halos = [moved(edges[c], 0) for c in range(CHUNKS)]
    hi, lo, base, base_sums, choice = opened(dims, ticks, weights, in_flight, outcomes, prior_logp)
    shared = [choice, hi, lo]
    states = [(base, base_sums)] * CHUNKS
    mains = [None] * CHUNKS
    done = []
    for tick in range(ticks):
        for c in range(CHUNKS):
            if tick > 0:
                states[c] = near(dims, tick, ticks, c, shared, mains[c], entering)
            mains[c], other = far(dims, tick, ticks, c, shared, states[c], halos[c], entering, done)
            if tick == ticks - 1:
                done = [other]
                continue
            mains[c] = lax.ppermute(mains[c], "site", up)
            halos[c] = moved(other, 1)
    parts = sector_terms(done[0], sectors)
    return tuple(finish(mains, parts, ticks, span * sectors))


def solution(mesh):
    sizes = (mesh.shape["site"], mesh.shape["sector"])

    def whole(site_tensor, outcomes, *others):
        call = jax.shard_map(
            functools.partial(per_device, *sizes),
            mesh=mesh,
            in_specs=(
                P("site", None, "sector", None, None),
                P(None, "site", None),
                P("site", None, "sector"),
                P("site", None),
                P(None, None, "sector"),
            ),
            out_specs=(P("site", None, "sector"), P("site", None)),
            check_vma=False,
        )
        return call(site_tensor, outcomes, *others)

    return whole
```
